256 devices in a mesh: dp: 4 (over y), sx: 4 (over x_lo, core), sy: 16 (over z, x_hi).
Axes of the slice: x: 4 (x_hi: 2, x_lo: 2; x = x_hi * 2 + x_lo), y: 4, z: 8, core: 2. Of those that a mesh axis runs over, the one named last changes fastest.
Arguments:
- features: bfloat16 [4, 4, 16, 3072, 128], P('dp', 'sx', 'sy'), may hold values from -6 to 6
- cotangent: bfloat16 [4, 4, 16, 3072, 128], P('dp', 'sx', 'sy'), may hold values from -6 to 6
- weights: bfloat16 [27, 128, 128], replicated, may hold values from -0.109375 to 0.109375
- tables: int32 [4, 4, 16, 27, 24], P('dp', 'sx', 'sy'), may hold values from 0 to 56, as said below
- send_lists: int32 [4, 4, 16, 4], P('dp', 'sx', 'sy'), may hold values from 0 to 23, as said below
- counts: int32 [4, 4, 16], P('dp', 'sx', 'sy'), may hold values from 6 to 24, as said below
Outputs:
- output: bfloat16 [4, 4, 16, 3072, 128], P('dp', 'sx', 'sy')
- input_grad: bfloat16 [4, 4, 16, 3072, 128], P('dp', 'sx', 'sy')
- weight_grad: float32 [27, 128, 128], replicated
The draws below stay inside these ranges and needn't reach their ends.
Inputs may be any that keep to these rules, and one draw needn't show every extreme that they name: `tables`: entries below 24 name a block of the tile, 24 + n * 4 + s' the s'-th sent block of neighbour direction n, 56 the empty block; under offset 27 // 2 every block reads itself. `send_lists`: the 4 blocks of one tile are distinct. `counts`: some tile has all 24 blocks active.
All inputs are finite; a program needn't handle non-finite values.
Results may differ from the reference program's by a relative error of at most 0.001.
Values may be sent and summed in bfloat16 or wider, within the bound.
A program may use at most 64 MiB of HBM per device.

```python
import math
import jax
import jax.numpy as jnp
from jax import lax

C = 128
K = 27
BV = 128
NB = 24
NS = 4
SCENES = 4
TX = 4
TY = 16
VOX = 3072
NE = 57
TOTAL_VOX = 786432


def draw_tables(key, part):
    key_kind, key_local, key_halo = jax.random.split(key, 3)
    shape = (SCENES, TX, TY, K, NB)
    kinds = jax.random.randint(key_kind, shape, 0, 10)
    local_pick = jax.random.randint(key_local, shape, 0, NB)
    halo_pick = NB + jax.random.randint(key_halo, shape, 0, 8 * NS)
    empty_pick = jnp.full(shape, NB + 8 * NS, jnp.int32)
    picks = jnp.where(kinds < 5, local_pick, jnp.where(kinds < 8, halo_pick, empty_pick))
    centre = jnp.broadcast_to(jnp.arange(NB, dtype=jnp.int32), shape)
    offset_ids = jnp.broadcast_to(jnp.arange(K, dtype=jnp.int32)[:, None], shape)
    picks = jnp.where(offset_ids == K // 2, centre, picks)
    return picks.astype(jnp.int32)


def draw_send_lists(key, part):
    scores = jax.random.randint(key, (SCENES, TX, TY, NB), 0, 4096) * NB + jnp.arange(NB, dtype=jnp.int32)
    order = jnp.argsort(scores, axis=-1, stable=True)
    return order[..., :NS].astype(jnp.int32)


def draw_counts(key, part):
    key_count, key_full = jax.random.split(key, 2)
    shape = (SCENES, TX, TY)
    values = jax.random.randint(key_count, shape, max(NB // 4, 1), NB + 1)
    full_tile = jax.random.randint(key_full, (), 0, SCENES * TX * TY)
    tile_ids = jnp.arange(SCENES * TX * TY, dtype=jnp.int32).reshape(shape)
    return jnp.where(tile_ids == full_tile, NB, values).astype(jnp.int32)


def shard_levels(own_key, shape, cuts, smallest, largest):
    def one(dim, shards_of):
        steps = jax.random.uniform(jax.random.fold_in(jax.random.fold_in(own_key, 6), dim), (shards_of,), jnp.float32, smallest / len(cuts), largest / len(cuts))
        return jnp.repeat(jnp.exp(steps), shape[dim] // shards_of).reshape((-1,) + (1,) * (len(shape) - dim - 1))

    loudness = one(*cuts[0])
    for cut in cuts[1:]:
        loudness = loudness * one(*cut)
    return loudness


def scatter_about(key, shape, deviation, bound, cuts=(), kind=jnp.bfloat16):
    factor_of = shard_levels(key, shape, cuts, -0.22, 0.18) if cuts else 1.0
    array = jax.random.normal(key, shape, jnp.float32) * deviation * factor_of
    return jnp.minimum(jnp.maximum(array, -bound), bound).astype(kind)


def setup_inputs(seed: int = 0) -> dict:
    splits = jax.random.split(jax.random.key(seed), 7)
    return {
        "features": scatter_about(splits[0], (SCENES, TX, TY, VOX, C), 1.0, 6.0, ((0, 4), (1, 4), (2, 16))),
        "cotangent": scatter_about(splits[1], (SCENES, TX, TY, VOX, C), 1.0, 6.0, ((0, 4), (1, 4), (2, 16))),
        "weights": scatter_about(splits[2], (K, C, C), (K * C) ** -0.5, 0.109375),
        "tables": draw_tables(jax.random.fold_in(splits[6], 71), 0),
        "send_lists": draw_send_lists(jax.random.fold_in(splits[6], 71), 0),
        "counts": draw_counts(jax.random.fold_in(splits[6], 71), 0),
    }


directions = ((-1, -1), (-1, 0), (-1, 1), (0, -1), (0, 1), (1, -1), (1, 0), (1, 1))

def device_pass(weight_sum, item):
    extended, blocks_grad, offset_table, weights = item
    weight_full = weights.astype(jnp.float32)
    gathered = extended[offset_table].astype(jnp.float32)
    grad_full = blocks_grad.astype(jnp.float32)
    hp = lax.Precision.HIGHEST
    outputs = jnp.einsum('kovc,kcd->ovd', gathered, weight_full, precision=hp)
    weight_part = jnp.einsum('kovc,ovd->kcd', gathered, grad_full, precision=hp)
    contrib = jnp.einsum('ovd,kcd->kovc', grad_full, weight_full, precision=hp)
    grad_ext = jnp.zeros((NE, BV, C), jnp.float32).at[offset_table.reshape(-1)].add(contrib.reshape(K * NB, BV, C))
    return (weight_sum + weight_part, (outputs, grad_ext))

def add_back(local_grad, sent_ids, portion):
    return local_grad.at[sent_ids].add(portion)

def reference(features, cotangent, weights, tables, send_lists, counts):
    devices = SCENES * TX * TY
    active = (jnp.arange(NB)[None, None, None, :] < counts[..., None]).astype(jnp.bfloat16)[..., None, None]
    blocks_in = features.reshape(SCENES, TX, TY, NB, BV, C) * active
    blocks_grad = cotangent.reshape(SCENES, TX, TY, NB, BV, C) * active
    sent = jnp.take_along_axis(blocks_in, send_lists[..., None, None], axis=3)
    padded = jnp.pad(sent, ((0, 0), (1, 1), (1, 1), (0, 0), (0, 0), (0, 0)))
    neighbours = [padded[:, 1 + step_x:1 + step_x + TX, 1 + step_y:1 + step_y + TY] for step_x, step_y in directions]
    extended = jnp.concatenate([blocks_in] + neighbours + [jnp.zeros((SCENES, TX, TY, 1, BV, C), jnp.bfloat16)], axis=3)
    weight_stack = jnp.broadcast_to(weights[None], (devices, K, C, C))
    weight_sum, (outputs, grad_ext) = lax.scan(device_pass, jnp.zeros((K, C, C), jnp.float32), (extended.reshape(devices, NE, BV, C), blocks_grad.reshape(devices, NB, BV, C), tables.reshape(devices, K, NB), weight_stack))
    active_full = active.astype(jnp.float32)
    output = (outputs.reshape(SCENES, TX, TY, NB, BV, C) * active_full).astype(jnp.bfloat16).reshape(features.shape)
    grad_ext = grad_ext.reshape(SCENES, TX, TY, NE, BV, C)
    halo_grads = grad_ext[:, :, :, NB:NB + 8 * NS].reshape(SCENES, TX, TY, 8, NS, BV, C)
    halo_padded = jnp.pad(halo_grads, ((0, 0), (1, 1), (1, 1), (0, 0), (0, 0), (0, 0), (0, 0)))
    returned = jnp.zeros((SCENES, TX, TY, NS, BV, C), jnp.float32)
    for slot_index, (step_x, step_y) in enumerate(directions):
        returned = returned + halo_padded[:, 1 - step_x:1 - step_x + TX, 1 - step_y:1 - step_y + TY, slot_index]
    local_grad = jax.vmap(add_back)(grad_ext[:, :, :, :NB].reshape(devices, NB, BV, C), send_lists.reshape(devices, NS), returned.reshape(devices, NS, BV, C))
    input_grad = (local_grad.reshape(SCENES, TX, TY, NB, BV, C) * active_full).astype(jnp.bfloat16).reshape(features.shape)
    weight_grad = weight_sum * (1.0 / math.sqrt(TOTAL_VOX))
    return (output, input_grad, weight_grad)
```

```python
import functools
import math

import jax
import jax.numpy as jnp
from jax import lax
from jax.experimental import pallas as pl
from jax.experimental.pallas import tpu as pltpu
from jax.sharding import PartitionSpec as P

MESH = pl.DeviceIdType.MESH
F32 = jnp.float32
BF16 = jnp.bfloat16


def scatter_body(tables, sends, counts, feats, cot, weights, outgoing, grad_ext, grads, turned):
    num_blocks, rows, channels = cot.shape
    offsets = weights.shape[0]
    pairs = offsets // 2
    group = 4 if num_blocks % 4 == 0 else num_blocks
    count = counts[0, 0]

    grad_ext[...] = jnp.zeros_like(grad_ext)
    for s in range(outgoing.shape[0]):
        block = sends[0, s]
        outgoing[s] = jnp.where(block < count, feats[block], jnp.zeros((rows, channels), BF16))
    for b in range(num_blocks):
        grads[b] = jnp.where(b < count, cot[b], jnp.zeros((rows, channels), BF16))

    def turn(k, carry):
        turned[k] = weights[k].T
        return carry

    lax.fori_loop(0, offsets, turn, 0)

    def pair(p, carry):
        both = jnp.concatenate([turned[2 * p], turned[2 * p + 1]], axis=1)
        for first in range(0, num_blocks, group):
            lhs = grads[first : first + group].reshape(group * rows, channels)
            terms = jnp.dot(lhs, both, preferred_element_type=F32)
            for i in range(group):
                term = terms[i * rows : (i + 1) * rows]
                grad_ext[tables[first + i, 2 * p]] += term[:, :channels]
                grad_ext[tables[first + i, 2 * p + 1]] += term[:, channels:]
        return carry

    lax.fori_loop(0, pairs, pair, 0)
    for k in range(2 * pairs, offsets):
        for first in range(0, num_blocks, group):
            lhs = grads[first : first + group].reshape(group * rows, channels)
            terms = jnp.dot(lhs, turned[k], preferred_element_type=F32)
            for i in range(group):
                grad_ext[tables[first + i, k]] += terms[i * rows : (i + 1) * rows]


def main_body(
    sizes,
    tables,
    sends,
    counts,
    feats,
    cot,
    weights,
    outgoing,
    grad_ext,
    out_hbm,
    grad_hbm,
    weight_hbm,
    ext,
    turned,
    grads,
    taps,
    own_grad,
    from_x,
    to_y,
    from_y,
    returned,
    part,
    from_core,
    from_plane,
    plane_sum,
    from_z,
    plane_full,
    full,
    total,
    out_block,
    grad_block,
    in_sem,
    out_sem,
    fy_send,
    fy_recv,
    fx_send,
    fx_recv,
    bx_send,
    bx_recv,
    by_send,
    by_recv,
    c_send,
    c_recv,
    p_send,
    p_recv,
    z_send,
    z_recv,
    gz_send,
    gz_recv,
    gp_send,
    gp_recv,
    gc_send,
    gc_recv,
):
    n_y, n_sx, n_sy = sizes
    n_lo, n_hi, n_z = n_sx // 2, 2, n_sy // 2
    n_x = n_lo * n_hi
    n_plane = n_x * n_y
    num_blocks, rows, channels = cot.shape
    offsets = weights.shape[0]
    num_sent = outgoing.shape[0]
    half = part.shape[0] // 2
    piece = channels // n_plane
    z_depth = from_z.shape[1]
    count = counts[0, 0]

    y, sx, sy = lax.axis_index("dp"), lax.axis_index("sx"), lax.axis_index("sy")
    core, lo, hi, z = lax.rem(sx, 2), sx // 2, lax.rem(sy, 2), sy // 2
    here = y * n_x + hi * n_lo + lo

    def device(dp, x, t):
        return {"dp": dp, "sx": x, "sy": t}

    def plane_device(p):
        py, px = p // n_x, lax.rem(p, n_x)
        return device(py, lax.rem(px, n_lo) * 2 + core, z * 2 + px // n_lo)

    def z_device(level):
        return device(y, sx, level * 2 + hi)

    partner = device(y, sx + 1 - 2 * core, sy)
    west, east = device(y, sx - 1, sy), device(y, sx + 1, sy)
    south, north = device(y, sx, sy - 1), device(y, sx, sy + 1)
    has_west, has_east = sx > 0, sx < n_sx - 1
    has_south, has_north = sy > 0, sy < n_sy - 1

    barrier = pltpu.get_barrier_semaphore()
    for there, target in (
        (has_west, west),
        (has_east, east),
        (has_south, south),
        (has_north, north),
    ):

        @pl.when(there)
        def _():
            pl.semaphore_signal(barrier, inc=1, device_id=target, device_id_type=MESH)

    pl.semaphore_signal(barrier, inc=1, device_id=partner, device_id_type=MESH)

    def greet_plane(d, carry):
        target = plane_device(lax.rem(here + d, n_plane))
        pl.semaphore_signal(barrier, inc=1, device_id=target, device_id_type=MESH)
        return carry

    def greet_z(d, carry):
        target = z_device(lax.rem(z + d, n_z))
        pl.semaphore_signal(barrier, inc=1, device_id=target, device_id_type=MESH)
        return carry

    lax.fori_loop(1, n_plane, greet_plane, 0)
    lax.fori_loop(1, n_z, greet_z, 0)

    loads = [
        pltpu.make_async_copy(feats, ext.at[pl.ds(0, num_blocks)], in_sem.at[0]),
        pltpu.make_async_copy(cot, grads, in_sem.at[1]),
        pltpu.make_async_copy(weights, taps.at[pl.ds(0, offsets)], in_sem.at[2]),
        pltpu.make_async_copy(grad_ext.at[pl.ds(0, num_blocks)], own_grad, in_sem.at[3]),
    ]
    for load in loads:
        load.start()

    greeters = n_plane + n_z - 1
    greeters = greeters + jnp.where(has_west, 1, 0) + jnp.where(has_east, 1, 0)
    greeters = greeters + jnp.where(has_south, 1, 0) + jnp.where(has_north, 1, 0)
    pl.semaphore_wait(barrier, greeters)

    def remote(src, dst, send, recv, target):
        return pltpu.make_async_remote_copy(
            src_ref=src,
            dst_ref=dst,
            send_sem=send,
            recv_sem=recv,
            device_id=target,
            device_id_type=MESH,
        )

    base = num_blocks

    def slots(n):
        return ext.at[pl.ds(base + n * num_sent, num_sent)]

    to_north = remote(outgoing, slots(3), fy_send.at[0], fy_recv.at[0], north)
    to_south = remote(outgoing, slots(4), fy_send.at[1], fy_recv.at[1], south)
    to_east = [
        remote(outgoing, slots(1), fx_send.at[0], fx_recv.at[0], east),
        remote(slots(3), slots(0), fx_send.at[1], fx_recv.at[1], east),
        remote(slots(4), slots(2), fx_send.at[2], fx_recv.at[2], east),
    ]
    to_west = [
        remote(outgoing, slots(6), fx_send.at[3], fx_recv.at[3], west),
        remote(slots(3), slots(5), fx_send.at[4], fx_recv.at[4], west),
        remote(slots(4), slots(7), fx_send.at[5], fx_recv.at[5], west),
    ]
    grads_west = remote(
        grad_ext.at[pl.ds(base, 3 * num_sent)], from_x.at[1], bx_send.at[0], bx_recv.at[0], west
    )
    grads_east = remote(
        grad_ext.at[pl.ds(base + 5 * num_sent, 3 * num_sent)],
        from_x.at[0],
        bx_send.at[1],
        bx_recv.at[1],
        east,
    )

    @pl.when(has_north)
    def _():
        to_north.start()

    @pl.when(has_south)
    def _():
        to_south.start()

    @pl.when(has_east)
    def _():
        to_east[0].start()

    @pl.when(has_west)
    def _():
        to_west[0].start()

    zeros = jnp.zeros((rows, channels), BF16)
    sent_zeros = jnp.zeros((num_sent, rows, channels), BF16)

    def clear(n):
        ext[base + n * num_sent : base + (n + 1) * num_sent] = sent_zeros

    @pl.when(jnp.logical_not(has_south))
    def _():
        clear(3)
        clear(0)
        clear(5)

    @pl.when(jnp.logical_not(has_north))
    def _():
        clear(4)
        clear(2)
        clear(7)

    @pl.when(jnp.logical_not(has_west))
    def _():
        clear(1)

        @pl.when(has_south)
        def _():
            clear(0)

        @pl.when(has_north)
        def _():
            clear(2)

    @pl.when(jnp.logical_not(has_east))
    def _():
        clear(6)

        @pl.when(has_south)
        def _():
            clear(5)

        @pl.when(has_north)
        def _():
            clear(7)

    empty = base + 8 * num_sent
    ext[empty] = zeros
    turned[empty] = zeros
    taps[offsets] = jnp.zeros((channels, channels), BF16)
    returned[num_sent] = jnp.zeros((rows, channels), F32)

    loads[0].wait()
    for b in range(num_blocks):
        block = jnp.where(b < count, ext[b], zeros)
        ext[b] = block
        turned[b] = block.T
    loads[1].wait()
    for b in range(num_blocks):
        grads[b] = jnp.where(b < count, grads[b], zeros)

    @pl.when(has_south)
    def _():
        to_north.wait_recv()

        @pl.when(has_east)
        def _():
            to_east[1].start()

        @pl.when(has_west)
        def _():
            to_west[1].start()

    @pl.when(has_north)
    def _():
        to_south.wait_recv()

        @pl.when(has_east)
        def _():
            to_east[2].start()

        @pl.when(has_west)
        def _():
            to_west[2].start()

    @pl.when(has_east)
    def _():
        grads_east.start()

    @pl.when(has_west)
    def _():
        grads_west.start()

    def turn(n):
        for s in range(num_sent):
            turned[base + n * num_sent + s] = ext[base + n * num_sent + s].T

    turn(3)
    turn(4)

    @pl.when(has_west)
    def _():
        to_east[0].wait_recv()

        @pl.when(has_south)
        def _():
            to_east[1].wait_recv()

        @pl.when(has_north)
        def _():
            to_east[2].wait_recv()

    @pl.when(has_east)
    def _():
        to_west[0].wait_recv()

        @pl.when(has_south)
        def _():
            to_west[1].wait_recv()

        @pl.when(has_north)
        def _():
            to_west[2].wait_recv()

    for n in (0, 1, 2, 5, 6, 7):
        turn(n)

    chunk = half // 2

    def weight_terms(first):
        def step(pair, carry):
            rhs = grads[pl.ds(2 * pair, 2)].reshape(2 * rows, channels)
            parts = []
            for i in range(chunk):
                k = jnp.minimum(first + i, offsets - 1)
                parts.append(
                    jnp.concatenate(
                        [turned[tables[2 * pair, k]], turned[tables[2 * pair + 1, k]]], axis=1
                    )
                )
            lhs = jnp.concatenate(parts, axis=0)
            terms = jnp.dot(lhs, rhs, preferred_element_type=F32)
            part[pl.ds(first, chunk)] += terms.reshape(chunk, channels, channels)
            return carry

        part[pl.ds(first, chunk)] = jnp.zeros((chunk, channels, channels), F32)
        lax.fori_loop(0, num_blocks // 2, step, 0)

    own, other = core * half, (1 - core) * half
    to_core = []
    for c in range(2):
        weight_terms(other + c * chunk)
        copy = remote(
            part.at[pl.ds(other + c * chunk, chunk)],
            from_core.at[pl.ds(c * chunk, chunk)],
            c_send.at[c],
            c_recv.at[c],
            partner,
        )
        copy.start()
        to_core.append(copy)

    def from_sides(q):
        where = pl.ds((q + 1) * num_sent, num_sent)
        return (from_x.at[0, where], from_x.at[1, where])

    @pl.when(has_west)
    def _():
        grads_east.wait_recv()

    @pl.when(has_east)
    def _():
        grads_west.wait_recv()

    @pl.when(jnp.logical_not(has_west))
    def _():
        from_x[0] = jnp.zeros_like(from_x[0])

    @pl.when(jnp.logical_not(has_east))
    def _():
        from_x[1] = jnp.zeros_like(from_x[1])

    own_halo = [
        pltpu.make_async_copy(
            grad_ext.at[pl.ds(base + (3 + i) * num_sent, num_sent)], to_y.at[i], in_sem.at[4 + i]
        )
        for i in range(2)
    ]
    for load in own_halo:
        load.start()
    for i, q in enumerate((-1, 1)):
        own_halo[i].wait()
        left, right = from_sides(q)
        to_y[i] = to_y[i] + left[...] + right[...]
    sums_south = remote(to_y.at[0], from_y.at[1], by_send.at[0], by_recv.at[0], south)
    sums_north = remote(to_y.at[1], from_y.at[0], by_send.at[1], by_recv.at[1], north)

    @pl.when(has_south)
    def _():
        sums_south.start()

    @pl.when(has_north)
    def _():
        sums_north.start()

    for c in range(2):
        weight_terms(own + c * chunk)
    for c in range(2):
        to_core[c].wait_recv()
        part[pl.ds(own + c * chunk, chunk)] += from_core[c * chunk : (c + 1) * chunk]

    def plane_copy(d):
        p = lax.rem(here + d, n_plane)
        src = part.at[pl.ds(own, half), pl.ds(pl.multiple_of(p * piece, piece), piece)]
        return remote(src, from_plane.at[d - 1], p_send.at[d - 1], p_recv.at[d - 1], plane_device(p))

    def plane_start(d, carry):
        plane_copy(d).start()
        return carry

    lax.fori_loop(1, n_plane, plane_start, 0)

    loads[2].wait()
    group = 8 if num_blocks % 8 == 0 else num_blocks
    for first in range(0, num_blocks, group):

        def step(pair, carry):
            rhs = taps[pl.ds(2 * pair, 2)].reshape(2 * channels, channels)
            other_k = jnp.minimum(2 * pair + 1, offsets - 1)
            parts = []
            for i in range(group):
                parts.append(
                    jnp.concatenate(
                        [ext[tables[first + i, 2 * pair]], ext[tables[first + i, other_k]]], axis=1
                    )
                )
            lhs = jnp.concatenate(parts, axis=0)
            terms = jnp.dot(lhs, rhs, preferred_element_type=F32)
            total[...] += terms.reshape(group, rows, channels)
            return carry

        total[...] = jnp.zeros_like(total)
        lax.fori_loop(0, (offsets + 1) // 2, step, 0)
        for i in range(group):
            b = first + i
            out_block[b] = jnp.where(b < count, total[i], jnp.zeros((rows, channels), F32)).astype(
                BF16
            )
    out_copy = pltpu.make_async_copy(out_block, out_hbm, out_sem.at[0])
    out_copy.start()

    returned_sum = from_x[0, num_sent : 2 * num_sent] + from_x[1, num_sent : 2 * num_sent]
    returned[0:num_sent] = returned_sum

    @pl.when(has_south)
    def _():
        sums_north.wait_recv()
        returned[0:num_sent] += from_y[0]

    @pl.when(has_north)
    def _():
        sums_south.wait_recv()
        returned[0:num_sent] += from_y[1]

    loads[3].wait()
    for b in range(num_blocks):
        slot = num_sent
        for s in range(num_sent):
            slot = jnp.where(sends[0, s] == b, s, slot)
        value = own_grad[b] + returned[slot]
        grad_block[b] = jnp.where(b < count, value, jnp.zeros((rows, channels), F32)).astype(BF16)
    grad_copy = pltpu.make_async_copy(grad_block, grad_hbm, out_sem.at[1])
    grad_copy.start()

    if plane_sum.shape[0] > half:
        plane_sum[half:] = jnp.zeros((plane_sum.shape[0] - half, piece, channels), F32)
    plane_sum[0:half] = part[pl.ds(own, half), pl.ds(pl.multiple_of(here * piece, piece), piece)]

    def plane_add(d, carry):
        plane_copy(d).wait_recv()
        plane_sum[0:half] += from_plane[d - 1]
        return carry

    lax.fori_loop(1, n_plane, plane_add, 0)

    def z_copy(d):
        level = lax.rem(z + d, n_z)
        src = plane_sum.at[pl.ds(level * z_depth, z_depth)]
        return remote(src, from_z.at[d - 1], z_send.at[d - 1], z_recv.at[d - 1], z_device(level))

    def z_start(d, carry):
        z_copy(d).start()
        return carry

    lax.fori_loop(1, n_z, z_start, 0)
    mine = pl.ds(z * z_depth, z_depth)
    plane_full[mine] = plane_sum[mine]

    def z_add(d, carry):
        z_copy(d).wait_recv()
        plane_full[mine] += from_z[d - 1]
        return carry

    lax.fori_loop(1, n_z, z_add, 0)

    def gather_z_copy(d):
        level = lax.rem(z + d, n_z)
        return remote(
            plane_full.at[mine],
            plane_full.at[mine],
            gz_send.at[d - 1],
            gz_recv.at[d - 1],
            z_device(level),
        )

    def gather_z_wait(d):
        level = lax.rem(z - d + n_z, n_z)
        there = pl.ds(level * z_depth, z_depth)
        remote(
            plane_full.at[there],
            plane_full.at[there],
            gz_send.at[d - 1],
            gz_recv.at[d - 1],
            z_device(level),
        ).wait_recv()

    def gather_z_start(d, carry):
        gather_z_copy(d).start()
        return carry

    def gather_z_end(d, carry):
        gather_z_wait(d)
        return carry

    lax.fori_loop(1, n_z, gather_z_start, 0)
    lax.fori_loop(1, n_z, gather_z_end, 0)

    def full_piece(p):
        return full.at[pl.ds(own, half), pl.ds(pl.multiple_of(p * piece, piece), piece)]

    def gather_plane_copy(d):
        target = plane_device(lax.rem(here + d, n_plane))
        return remote(
            plane_full.at[pl.ds(0, half)],
            full_piece(here),
            gp_send.at[d - 1],
            gp_recv.at[d - 1],
            target,
        )

    def gather_plane_start(d, carry):
        gather_plane_copy(d).start()
        return carry

    lax.fori_loop(1, n_plane, gather_plane_start, 0)
    full[pl.ds(own, half), pl.ds(pl.multiple_of(here * piece, piece), piece)] = plane_full[0:half]

    def core_copy(d):
        p = lax.rem(here - d + n_plane, n_plane)
        return remote(full_piece(p), full_piece(p), gc_send.at[d], gc_recv.at[d], partner)

    def core_wait(d):
        p = lax.rem(here - d + n_plane, n_plane)
        where = full.at[pl.ds(other, half), pl.ds(pl.multiple_of(p * piece, piece), piece)]
        remote(where, where, gc_send.at[d], gc_recv.at[d], partner).wait_recv()

    core_copy(0).start()

    def gather_plane_end(d, carry):
        p = lax.rem(here - d + n_plane, n_plane)
        remote(
            full_piece(p), full_piece(p), gp_send.at[d - 1], gp_recv.at[d - 1], plane_device(p)
        ).wait_recv()
        core_copy(d).start()
        return carry

    lax.fori_loop(1, n_plane, gather_plane_end, 0)
    own_copy = pltpu.make_async_copy(
        full.at[pl.ds(own, half)], weight_hbm.at[pl.ds(own, half)], out_sem.at[2]
    )
    own_copy.start()

    def core_end(d, carry):
        core_wait(d)
        return carry

    lax.fori_loop(0, n_plane, core_end, 0)
    other_copy = pltpu.make_async_copy(
        full.at[pl.ds(other, half)], weight_hbm.at[pl.ds(other, half)], out_sem.at[3]
    )
    other_copy.start()

    for there, copies in (
        (has_north, [to_north, sums_north]),
        (has_south, [to_south, sums_south]),
        (has_east, [to_east[0], grads_east]),
        (has_west, [to_west[0], grads_west]),
        (jnp.logical_and(has_east, has_south), [to_east[1]]),
        (jnp.logical_and(has_east, has_north), [to_east[2]]),
        (jnp.logical_and(has_west, has_south), [to_west[1]]),
        (jnp.logical_and(has_west, has_north), [to_west[2]]),
    ):

        @pl.when(there)
        def _():
            for copy in copies:
                copy.wait_send()

    for copy in to_core:
        copy.wait_send()

    def plane_drain(d, carry):
        plane_copy(d).wait_send()
        gather_plane_copy(d).wait_send()
        core_copy(d).wait_send()
        return carry

    def z_drain(d, carry):
        z_copy(d).wait_send()
        gather_z_copy(d).wait_send()
        return carry

    core_copy(0).wait_send()
    lax.fori_loop(1, n_plane, plane_drain, 0)
    lax.fori_loop(1, n_z, z_drain, 0)
    for copy in (out_copy, grad_copy, own_copy, other_copy):
        copy.wait()


def local(sizes, features, cotangent, weights, tables, send_lists, counts):
    num_blocks = tables.shape[4]
    num_sent = send_lists.shape[3]
    offsets, channels = weights.shape[0], weights.shape[1]
    rows = features.shape[3] // num_blocks
    num_ext = num_blocks + 8 * num_sent + 1
    n_y, n_sx, n_sy = sizes
    n_plane, n_z = n_y * n_sx, n_sy // 2
    half = 2 * -(-offsets // 4)
    z_depth = -(-half // n_z)
    piece = channels // n_plane

    feats = features.reshape(num_blocks, rows, channels)
    cot = cotangent.reshape(num_blocks, rows, channels)
    table = tables.reshape(offsets, num_blocks).T
    sends = send_lists.reshape(1, num_sent)
    count = counts.reshape(1, 1)
    smem = pl.BlockSpec(memory_space=pltpu.SMEM)
    vmem = pl.BlockSpec(memory_space=pltpu.VMEM)
    anywhere = pl.BlockSpec(memory_space=pl.ANY)
    block = (rows, channels)

    outgoing, grad_ext = pl.pallas_call(
        scatter_body,
        out_shape=(
            jax.ShapeDtypeStruct((num_sent,) + block, BF16),
            jax.ShapeDtypeStruct((num_ext,) + block, F32),
        ),
        in_specs=[smem, smem, smem, vmem, vmem, vmem],
        out_specs=(vmem, vmem),
        scratch_shapes=[
            pltpu.VMEM((num_blocks,) + block, BF16),
            pltpu.VMEM((offsets, channels, channels), BF16),
        ],
        compiler_params=pltpu.CompilerParams(vmem_limit_bytes=40 << 20),
        name="scatter",
    )(table, sends, count, feats, cot, weights)

    dma = pltpu.SemaphoreType.DMA
    output, input_grad, weight_sum = pl.pallas_call(
        functools.partial(main_body, sizes),
        out_shape=(
            jax.ShapeDtypeStruct((num_blocks,) + block, BF16),
            jax.ShapeDtypeStruct((num_blocks,) + block, BF16),
            jax.ShapeDtypeStruct((2 * half, channels, channels), F32),
        ),
        in_specs=[smem, smem, smem] + [anywhere] * 5,
        out_specs=(anywhere,) * 3,
        scratch_shapes=[
            pltpu.VMEM((num_ext,) + block, BF16),
            pltpu.VMEM((num_ext, channels, rows), BF16),
            pltpu.VMEM((num_blocks,) + block, BF16),
            pltpu.VMEM((offsets + 1, channels, channels), BF16),
            pltpu.VMEM((num_blocks,) + block, F32),
            pltpu.VMEM((2, 3 * num_sent) + block, F32),
            pltpu.VMEM((2, num_sent) + block, F32),
            pltpu.VMEM((2, num_sent) + block, F32),
            pltpu.VMEM((num_sent + 1,) + block, F32),
            pltpu.VMEM((2 * half, channels, channels), F32),
            pltpu.VMEM((half, channels, channels), F32),
            pltpu.VMEM((n_plane - 1, half, piece, channels), F32),
            pltpu.VMEM((n_z * z_depth, piece, channels), F32),
            pltpu.VMEM((n_z - 1, z_depth, piece, channels), F32),
            pltpu.VMEM((n_z * z_depth, piece, channels), F32),
            pltpu.VMEM((2 * half, channels, channels), F32),
            pltpu.VMEM((8 if num_blocks % 8 == 0 else num_blocks,) + block, F32),
            pltpu.VMEM((num_blocks,) + block, BF16),
            pltpu.VMEM((num_blocks,) + block, BF16),
            dma((6,)),
            dma((4,)),
            dma((2,)),
            dma((2,)),
            dma((6,)),
            dma((6,)),
            dma((2,)),
            dma((2,)),
            dma((2,)),
            dma((2,)),
            dma((2,)),
            dma((2,)),
            dma((n_plane - 1,)),
            dma((n_plane - 1,)),
            dma((n_z - 1,)),
            dma((n_z - 1,)),
            dma((n_z - 1,)),
            dma((n_z - 1,)),
            dma((n_plane - 1,)),
            dma((n_plane - 1,)),
            dma((n_plane,)),
            dma((n_plane,)),
        ],
        compiler_params=pltpu.CompilerParams(
            collective_id=0, has_side_effects=True, vmem_limit_bytes=48 << 20
        ),
        name="main",
    )(table, sends, count, feats, cot, weights, outgoing, grad_ext)

    voxels = num_blocks * rows * n_y * n_sx * n_sy
    weight_grad = weight_sum[:offsets] * (1.0 / math.sqrt(voxels))
    return (output.reshape(features.shape), input_grad.reshape(features.shape), weight_grad)


def solution(mesh):
    sizes = tuple(mesh.shape[name] for name in ("dp", "sx", "sy"))
    return jax.shard_map(
        functools.partial(local, sizes),
        mesh=mesh,
        in_specs=(
            P("dp", "sx", "sy", None, None),
            P("dp", "sx", "sy", None, None),
            P(),
            P("dp", "sx", "sy", None, None),
            P("dp", "sx", "sy", None),
            P("dp", "sx", "sy"),
        ),
        out_specs=(P("dp", "sx", "sy", None, None), P("dp", "sx", "sy", None, None), P()),
        check_vma=False,
    )
```
